32 devices in a mesh: mp: 4 (over y, core), latent: 8 (over z, x).
Axes of the slice: x: 2, y: 2, z: 4, core: 2. Of those that a mesh axis runs over, the one named last changes fastest.
Arguments:
- resid_clean: bfloat16 [128, 4608], P(('mp', 'latent')), may hold values from -6 to 6
- resid_corrupt: bfloat16 [128, 4608], P(('mp', 'latent')), may hold values from -6 to 6
- answer_ids: int32 [128, 2], replicated, may hold values from 0 to 127, all different within a row
- unembed: bfloat16 [128, 4608], replicated, may hold values from -1.5 to 1.5
- pre_gain: float32 [4608], replicated, may hold values from 0.25 to 1.75
- post_gain: float32 [4608], replicated, may hold values from 0.25 to 1.75
- final_gain: float32 [4608], replicated, may hold values from 0.25 to 1.75
- w_gate: bfloat16 [4608, 36864], P(None, ('mp', 'latent')), may hold values from -0.09375 to 0.09375
- w_up: bfloat16 [4608, 36864], P(None, ('mp', 'latent')), may hold values from -0.09375 to 0.09375
- w_down: bfloat16 [36864, 4608], P(('mp', 'latent')), may hold values from -0.03125 to 0.03125
- w_enc: bfloat16 [4608, 65536], P(None, ('mp', 'latent')), may hold values from -0.09375 to 0.09375
- b_enc: float32 [65536], P(('mp', 'latent')), may hold values from -3 to 3
- w_dec: bfloat16 [65536, 4608], P(('mp', 'latent')), may hold values from -0.09375 to 0.09375
Outputs:
- attribution: float32 [1, 65536], P(None, ('mp', 'latent'))
The draws below stay inside these ranges and needn't reach their ends.
Inputs may be any that keep to these rules, and one draw needn't show every extreme that they name: `answer_ids`: the two indices of a token differ.
All inputs are finite; a program needn't handle non-finite values.
Results may differ from the reference program's by a relative error of at most 0.0056.
Values may be sent and summed in bfloat16 or wider, within the bound.
A program may use at most 128 MiB of HBM per device.

```python
import jax
import jax.numpy as jnp
from jax import lax

D = 4608
FF = 36864
LATENTS = 65536
CANDS = 128
SEQ = 128
PAIRS = 1
TOK = 128


def block_levels(stream_key, extent, cuts, low, largest):
    def one(position, parts):
        heights = jax.random.uniform(jax.random.fold_in(jax.random.fold_in(stream_key, 6), position), (parts,), jnp.float32, low / len(cuts), largest / len(cuts))
        return jnp.repeat(jnp.exp(heights), extent[position] // parts).reshape((-1,) + (1,) * (len(extent) - position - 1))

    gain = one(*cuts[0])
    for cut in cuts[1:]:
        gain = gain * one(*cut)
    return gain


def distinct(own_key, rows, number_of, top, lift):
    ranking = jax.random.permutation(jax.random.fold_in(own_key, 1), number_of)
    boost = ranking
    for power in range(3):
        boost = boost * boost // number_of
    boost = boost * lift // number_of
    chance = jax.random.randint(jax.random.fold_in(own_key, 2), (rows, number_of), 0, 4096) + boost
    sure = jax.random.permutation(jax.random.fold_in(own_key, 3), rows)[jnp.arange(number_of) % rows]
    chance = jnp.where(jnp.arange(rows)[:, None] == sure[None, :], 1 << 14, chance)
    score = chance * number_of + jnp.arange(number_of)
    return lax.top_k(score.astype(jnp.int32), top)[1].astype(jnp.int32)


def noise(own_key, extent, spread, bound, split=(), kind=jnp.bfloat16):
    level = block_levels(own_key, extent, split, -0.22, 0.18) if split else 1.0
    values = jax.random.normal(own_key, extent, jnp.float32) * spread * level
    return jnp.minimum(jnp.maximum(values, -bound), bound).astype(kind)


def setup_inputs(seed: int = 0) -> dict:
    keys = jax.random.split(jax.random.key(seed), 14)
    resid_clean = noise(keys[0], (TOK, D), 1.0, 6.0, ((0, 32),))
    resid_corrupt = noise(keys[1], (TOK, D), 1.0, 6.0, ((0, 32),))
    answer_ids = distinct(keys[2], TOK, CANDS, 2, 0)
    unembed = noise(keys[3], (CANDS, D), 0.25, 1.5)
    pre_gain = jnp.clip(1.0 + 0.15 * jax.random.normal(keys[4], (D,), jnp.float32), 0.25, 1.75)
    post_gain = jnp.clip(1.0 + 0.15 * jax.random.normal(keys[5], (D,), jnp.float32), 0.25, 1.75)
    final_gain = jnp.clip(1.0 + 0.15 * jax.random.normal(keys[6], (D,), jnp.float32), 0.25, 1.75)
    w_gate = noise(keys[7], (D, FF), D ** -0.5, 0.09375, ((1, 32),))
    w_up = noise(keys[8], (D, FF), D ** -0.5, 0.09375, ((1, 32),))
    w_down = noise(keys[9], (FF, D), FF ** -0.5, 0.03125, ((0, 32),))
    w_enc = noise(keys[10], (D, LATENTS), D ** -0.5, 0.09375, ((1, 32),))
    b_enc = noise(keys[11], (LATENTS,), 0.5, 3.0, ((0, 32),), jnp.float32)
    w_dec = noise(keys[12], (LATENTS, D), D ** -0.5, 0.09375, ((0, 32),))
    return {"resid_clean": resid_clean, "resid_corrupt": resid_corrupt, "answer_ids": answer_ids, "unembed": unembed, "pre_gain": pre_gain, "post_gain": post_gain, "final_gain": final_gain, "w_gate": w_gate, "w_up": w_up, "w_down": w_down, "w_enc": w_enc, "b_enc": b_enc, "w_dec": w_dec}


epsilon = 1e-06
gelu_scale = 0.7978845608028654
gelu_cubic = 0.044715

def gelu_tanh(value):
    return 0.5 * value * (1.0 + jnp.tanh(gelu_scale * (value + gelu_cubic * value * value * value)))

def gelu_slope(value):
    inner = jnp.tanh(gelu_scale * (value + gelu_cubic * value * value * value))
    return 0.5 * (1.0 + inner) + 0.5 * value * (1.0 - inner * inner) * gelu_scale * (1.0 + 3.0 * gelu_cubic * value * value)

def contract_last(left, right):
    return lax.dot_general(left, right, (((1,), (1,)), ((), ())), preferred_element_type=jnp.float32)

def output_grads(stream, mlp_out, answers, unembed, post_gain, final_gain):
    inv_post = lax.rsqrt(lax.optimization_barrier(jnp.mean(mlp_out * mlp_out, axis=-1, keepdims=True)) + epsilon)
    output = stream + mlp_out * inv_post * post_gain
    inv_final = lax.rsqrt(lax.optimization_barrier(jnp.mean(output * output, axis=-1, keepdims=True)) + epsilon)
    candidate = lax.broadcasted_iota(jnp.int32, (answers.shape[0], unembed.shape[0]), 1)
    selector = ((candidate == answers[:, 0:1]).astype(jnp.float32) - (candidate == answers[:, 1:2]).astype(jnp.float32)).astype(jnp.bfloat16)
    direction = jnp.dot(selector, unembed, preferred_element_type=jnp.float32)
    weighted = final_gain * direction
    grad_output = inv_final * weighted - output * (inv_final * inv_final * inv_final) * lax.optimization_barrier(jnp.mean(weighted * output, axis=-1, keepdims=True))
    post_grad = post_gain * grad_output
    grad_mlp = (inv_post * post_grad - mlp_out * (inv_post * inv_post * inv_post) * lax.optimization_barrier(jnp.mean(post_grad * mlp_out, axis=-1, keepdims=True))).astype(jnp.bfloat16)
    return (grad_output, grad_mlp)

def reference(resid_clean, resid_corrupt, answer_ids, unembed, pre_gain, post_gain, final_gain, w_gate, w_up, w_down, w_enc, b_enc, w_dec):
    stream = resid_clean.astype(jnp.float32)
    inv_pre = lax.rsqrt(lax.optimization_barrier(jnp.mean(stream * stream, axis=-1, keepdims=True)) + epsilon)
    normed = (stream * inv_pre * pre_gain).astype(jnp.bfloat16)
    gate_pre = jnp.dot(normed, w_gate, preferred_element_type=jnp.float32)
    up_proj = jnp.dot(normed, w_up, preferred_element_type=jnp.float32)
    activated = gelu_tanh(gate_pre)
    hidden = (activated * up_proj).astype(jnp.bfloat16)
    mlp_out = jnp.dot(hidden, w_down, preferred_element_type=jnp.float32)
    grad_output, grad_mlp = output_grads(stream, mlp_out, answer_ids, unembed, post_gain, final_gain)
    grad_hidden = contract_last(grad_mlp, w_down)
    grad_gate = (grad_hidden * up_proj * gelu_slope(gate_pre)).astype(jnp.bfloat16)
    grad_up = (grad_hidden * activated).astype(jnp.bfloat16)
    grad_normed = contract_last(grad_gate, w_gate) + contract_last(grad_up, w_up)
    pre_grad = pre_gain * grad_normed
    grad_stream = (grad_output + inv_pre * pre_grad - stream * (inv_pre * inv_pre * inv_pre) * lax.optimization_barrier(jnp.mean(pre_grad * stream, axis=-1, keepdims=True))).astype(jnp.bfloat16)
    clean_code = jax.nn.relu(jnp.dot(resid_clean, w_enc, preferred_element_type=jnp.float32) + b_enc)
    corrupt_code = jax.nn.relu(jnp.dot(resid_corrupt, w_enc, preferred_element_type=jnp.float32) + b_enc)
    change = clean_code - corrupt_code
    projected = contract_last(grad_stream, w_dec)
    product = change * projected
    return lax.optimization_barrier(jnp.sum(product.reshape(PAIRS, SEQ, LATENTS), axis=1))
```

```python
import functools

import jax
import jax.numpy as jnp
from jax import lax
from jax.experimental import pallas as pl
from jax.experimental.pallas import tpu as pltpu
from jax.sharding import PartitionSpec as P

SEQ = 128


epsilon = 1e-06
gelu_scale = 0.7978845608028654
gelu_cubic = 0.044715


def gelu_tanh(value):
    return 0.5 * value * (1.0 + jnp.tanh(gelu_scale * (value + gelu_cubic * value * value * value)))


def gelu_slope(value):
    inner = jnp.tanh(gelu_scale * (value + gelu_cubic * value * value * value))
    return 0.5 * (1.0 + inner) + 0.5 * value * (1.0 - inner * inner) * gelu_scale * (
        1.0 + 3.0 * gelu_cubic * value * value
    )


def contract_last(left, right):
    return lax.dot_general(
        left, right, (((1,), (1,)), ((), ())), preferred_element_type=jnp.float32
    )


def output_grads(stream, mlp_out, answers, unembed, post_gain, final_gain):
    inv_post = lax.rsqrt(jnp.mean(mlp_out * mlp_out, axis=-1, keepdims=True) + epsilon)
    output = stream + mlp_out * inv_post * post_gain
    inv_final = lax.rsqrt(jnp.mean(output * output, axis=-1, keepdims=True) + epsilon)
    candidate = lax.broadcasted_iota(jnp.int32, (answers.shape[0], unembed.shape[0]), 1)
    selector = (
        (candidate == answers[:, 0:1]).astype(jnp.float32)
        - (candidate == answers[:, 1:2]).astype(jnp.float32)
    ).astype(jnp.bfloat16)
    direction = jnp.dot(selector, unembed, preferred_element_type=jnp.float32)
    weighted = final_gain * direction
    grad_output = inv_final * weighted - output * (inv_final * inv_final * inv_final) * jnp.mean(
        weighted * output, axis=-1, keepdims=True
    )
    post_grad = post_gain * grad_output
    grad_mlp = (
        inv_post * post_grad
        - mlp_out
        * (inv_post * inv_post * inv_post)
        * jnp.mean(post_grad * mlp_out, axis=-1, keepdims=True)
    ).astype(jnp.bfloat16)
    return (grad_output, grad_mlp)


def local(
    resid_clean,
    resid_corrupt,
    answer_ids,
    unembed,
    pre_gain,
    post_gain,
    final_gain,
    w_gate,
    w_up,
    w_down,
    w_enc,
    b_enc,
    w_dec,
):
    own_rows = resid_clean.shape[0]
    clean_all, corrupt_all = (
        lax.all_gather(resid_clean, ("mp", "latent"), axis=0, tiled=True),
        lax.all_gather(resid_corrupt, ("mp", "latent"), axis=0, tiled=True),
    )
    total_rows = clean_all.shape[0]
    offset = lax.axis_index(("mp", "latent")) * own_rows
    stream = clean_all.astype(jnp.float32)
    inv_pre = lax.rsqrt(jnp.mean(stream * stream, axis=-1, keepdims=True) + epsilon)
    normed = (stream * inv_pre * pre_gain).astype(jnp.bfloat16)
    gate_pre = jnp.dot(normed, w_gate, preferred_element_type=jnp.float32)
    up_proj = jnp.dot(normed, w_up, preferred_element_type=jnp.float32)
    activated = gelu_tanh(gate_pre)
    hidden = (activated * up_proj).astype(jnp.bfloat16)
    stream_rows = lax.dynamic_slice_in_dim(stream, offset, own_rows, 0)
    inv_rows = lax.dynamic_slice_in_dim(inv_pre, offset, own_rows, 0)
    mlp_out = lax.psum(
        jnp.dot(hidden, w_down, preferred_element_type=jnp.float32), ("mp", "latent")
    )
    grad_output, grad_mlp = output_grads(
        stream, mlp_out, answer_ids, unembed, post_gain, final_gain
    )
    grad_hidden = contract_last(grad_mlp, w_down)
    grad_rows_out = lax.dynamic_slice_in_dim(grad_output, offset, own_rows, 0)
    grad_gate = (grad_hidden * up_proj * gelu_slope(gate_pre)).astype(jnp.bfloat16)
    grad_up = (grad_hidden * activated).astype(jnp.bfloat16)
    grad_normed = lax.psum_scatter(
        contract_last(grad_gate, w_gate) + contract_last(grad_up, w_up),
        ("mp", "latent"),
        scatter_dimension=0,
        tiled=True,
    )
    pre_grad = pre_gain * grad_normed
    grad_stream = (
        grad_rows_out
        + inv_rows * pre_grad
        - stream_rows
        * (inv_rows * inv_rows * inv_rows)
        * jnp.mean(pre_grad * stream_rows, axis=-1, keepdims=True)
    ).astype(jnp.bfloat16)
    clean_code = jax.nn.relu(jnp.dot(clean_all, w_enc, preferred_element_type=jnp.float32) + b_enc)
    corrupt_code = jax.nn.relu(
        jnp.dot(corrupt_all, w_enc, preferred_element_type=jnp.float32) + b_enc
    )
    change = clean_code - corrupt_code
    projected = contract_last(
        lax.all_gather(grad_stream, ("mp", "latent"), axis=0, tiled=True), w_dec
    )
    product = change * projected
    return jnp.sum(product.reshape(total_rows // SEQ, SEQ, product.shape[1]), axis=1)


MESH = pl.DeviceIdType.MESH
BF = jnp.bfloat16
F32 = jnp.float32


class Place:
    def __init__(self, depth):
        self.depth = depth
        self.mp = lax.axis_index("mp")
        self.lat = lax.axis_index("latent")
        self.c, self.y = self.mp % 2, self.mp // 2
        self.x, self.z = self.lat % 2, self.lat // 2
        self.core_peer = (self.y * 2 + 1 - self.c, self.lat)
        self.mp_y = (1 - self.y) * 2 + self.c
        self.y_peer = (self.mp_y, self.lat)
        self.x_peer = (self.mp, self.z * 2 + 1 - self.x)

    def z_peer(self, step):
        return (self.mp, ((self.z + step) % self.depth) * 2 + self.x)

    def greet(self):
        barrier = pltpu.get_barrier_semaphore()
        peers = [self.core_peer, self.y_peer, self.x_peer]
        peers += [self.z_peer(step) for step in range(1, self.depth)]
        for peer in peers:
            pl.semaphore_signal(barrier, inc=1, device_id=peer, device_id_type=MESH)
        pl.semaphore_wait(barrier, len(peers))


class Wires:
    def __init__(self, send, recv):
        self.send, self.recv, self.used = send, recv, 0

    def start(self, src, dst, peer):
        i = self.used
        self.used += 1
        copy = pltpu.make_async_remote_copy(
            src_ref=src, dst_ref=dst, send_sem=self.send.at[i], recv_sem=self.recv.at[i],
            device_id=peer, device_id_type=MESH,
        )
        copy.start()
        return copy


def finish(copies):
    for copy in copies:
        copy.wait()


def rows16(start):
    return pl.ds(pl.multiple_of(start, 16), 16)


def rows32(start):
    return pl.ds(pl.multiple_of(start, 32), 32)


def gather_blocks(at, wires, own, buf):
    depth = at.depth
    cut = (buf.shape[1] // 256) * 128
    half0, half1 = pl.ds(0, cut), pl.ds(cut, buf.shape[1] - cut)
    lane = ((at.c * 2 + at.y) * 2 + at.x) * depth
    quad = depth * 16
    mine = rows16((lane + at.z) * 16)
    group = pl.ds(pl.multiple_of(lane * 16, quad), quad)
    group_y = pl.ds(pl.multiple_of(((at.c * 2 + 1 - at.y) * 2 + at.x) * quad, quad), quad)
    pair = pl.ds(pl.multiple_of((at.c * 2 + at.y) * 2 * quad, quad), 2 * quad)
    side = pl.ds(pl.multiple_of(at.c * 4 * quad, quad), 4 * quad)
    first = [wires.start(own, buf.at[mine], at.z_peer(s)) for s in range(1, depth)]
    buf[mine, :] = own[...]
    finish(first)
    yield
    cx = wires.start(buf.at[group, half0], buf.at[group, half0], at.x_peer)
    cy = wires.start(buf.at[group, half1], buf.at[group, half1], at.y_peer)
    finish([cx, cy])
    yield
    cy = wires.start(buf.at[pair, half0], buf.at[pair, half0], at.y_peer)
    cx = wires.start(buf.at[group, half1], buf.at[group, half1], at.x_peer)
    cx2 = wires.start(buf.at[group_y, half1], buf.at[group_y, half1], at.x_peer)
    finish([cy, cx, cx2])
    yield
    finish([wires.start(buf.at[side], buf.at[side], at.core_peer)])


def gather_rows(at, wires, own, buf):
    depth = at.depth
    width = own.shape[1]
    half = buf.shape[1] // 2
    halves = (pl.ds(0, half), pl.ds(half, half))
    mine = rows16((at.mp * 2 + at.x) * 16)
    other = rows16((at.mp_y * 2 + at.x) * 16)
    both = rows32(at.mp * 32)
    both_y = rows32(at.mp_y * 32)
    spot = buf.at[mine, pl.ds(pl.multiple_of(at.z * width, 128), width)]
    first = [wires.start(own, spot, at.z_peer(s)) for s in range(1, depth)]
    buf[mine, pl.ds(pl.multiple_of(at.z * width, 128), width)] = own[...]
    finish(first)
    yield

    def share(rows, h, peer):
        spot = buf.at[rows, halves[h]]
        return wires.start(spot, spot, peer)

    finish([share(mine, 0, at.x_peer), share(mine, 1, at.y_peer)])
    yield
    core = [share(both, 0, at.core_peer)]
    step = [share(both, 0, at.y_peer), share(mine, 1, at.x_peer), share(other, 1, at.x_peer)]
    finish(step)
    yield
    core += [share(both_y, 0, at.core_peer), share(both, 1, at.core_peer), share(both_y, 1, at.core_peer)]
    finish(core)


def scatter_sum(at, wires, part, bufs, total):
    rc, s1, ry, s2a, rx, s2b, rx2, ry2, s3, rz = bufs
    depth = at.depth
    width = total.shape[1]
    half = part.shape[1] // 2
    h0, h1 = pl.ds(0, half), pl.ds(half, half)
    core = []
    for h in (h0, h1):
        for yy in range(2):
            core.append(wires.start(
                part.at[rows32((yy * 2 + 1 - at.c) * 32), h], rc.at[yy, :, h], at.core_peer))
    own16, peer16 = rows16(at.x * 16), rows16((1 - at.x) * 16)
    yield
    finish(core[:2])
    for yy in range(2):
        s1[yy, :, h0] = (part[rows32((yy * 2 + at.c) * 32), h0].astype(F32) + rc[yy, :, h0].astype(F32)).astype(BF)
    cy = wires.start(s1.at[1 - at.y, :, h0], ry, at.y_peer)
    finish(core[2:])
    for yy in range(2):
        s1[yy, :, h1] = (part[rows32((yy * 2 + at.c) * 32), h1].astype(F32) + rc[yy, :, h1].astype(F32)).astype(BF)
    cx = [wires.start(s1.at[yy, peer16, h1], rx.at[yy], at.x_peer) for yy in range(2)]
    yield
    finish([cy])
    s2a[...] = (s1[at.y, :, h0].astype(F32) + ry[...].astype(F32)).astype(BF)
    cx2 = wires.start(s2a.at[peer16], rx2, at.x_peer)
    finish(cx)
    for yy in range(2):
        s2b[yy] = (s1[yy, own16, h1].astype(F32) + rx[yy].astype(F32)).astype(BF)
    cy2 = wires.start(s2b.at[1 - at.y], ry2, at.y_peer)
    yield
    finish([cx2])
    s3[:, h0] = (s2a[own16, :].astype(F32) + rx2[...].astype(F32)).astype(BF)
    finish([cy2])
    s3[:, h1] = (s2b[at.y].astype(F32) + ry2[...].astype(F32)).astype(BF)
    last = []
    for s in range(1, depth):
        column = pl.multiple_of(((at.z + s) % depth) * width, 128)
        last.append(wires.start(s3.at[:, pl.ds(column, width)], rz.at[s - 1], at.z_peer(s)))
    yield
    finish(last)
    value = s3[:, pl.ds(pl.multiple_of(at.z * width, 128), width)].astype(F32)
    for s in range(1, depth):
        value = value + rz[s - 1].astype(F32)
    total[...] = value


def scatter_buffers(d, depth):
    half, width = d // 2, d // depth
    return [
        pltpu.VMEM((2, 32, d), BF), pltpu.VMEM((2, 32, d), BF), pltpu.VMEM((32, half), BF),
        pltpu.VMEM((32, half), BF), pltpu.VMEM((2, 16, half), BF), pltpu.VMEM((2, 16, half), BF),
        pltpu.VMEM((16, half), BF), pltpu.VMEM((16, half), BF), pltpu.VMEM((16, d), BF),
        pltpu.VMEM((depth - 1, 16, width), BF),
    ]


def share_stats(at, wires, sums, out, inbox):
    lane = lax.broadcasted_iota(jnp.int32, (16, 128), 1)
    packed = jnp.zeros((16, 128), F32)
    for i, value in enumerate(sums):
        packed = jnp.where(lane == i, value, packed)
    out[...] = packed
    finish([wires.start(out, inbox.at[s - 1], at.z_peer(s)) for s in range(1, at.depth)])
    for s in range(1, at.depth):
        packed = packed + inbox[s - 1]
    return [packed[:, i : i + 1] for i in range(len(sums))]


def row_sum(value):
    return jnp.sum(value, axis=-1, keepdims=True)


def run(steps):
    for _ in steps:
        pass


def middle(at, wires, total, stats, inbox, d, clean, answers, unembed, post_gain, final_gain):
    width = total.shape[1]
    rows = rows16((at.mp * 2 + at.x) * 16)
    columns = pl.ds(pl.multiple_of(at.z * width, 128), width)
    m = total[...]
    s = clean[rows, columns].astype(F32)
    pg = post_gain[:, columns]
    ids = answers[rows, :]
    candidate = lax.broadcasted_iota(jnp.int32, (16, unembed.shape[0]), 1)
    selector = (
        jnp.where(candidate == ids[:, 0:1], 1.0, 0.0) - jnp.where(candidate == ids[:, 1:2], 1.0, 0.0)
    ).astype(BF)
    direction = jnp.dot(selector, unembed[:, columns], preferred_element_type=F32)
    weighted = final_gain[:, columns] * direction
    mg = m * pg
    sums = [row_sum(m * m), row_sum(s * s), row_sum(s * mg), row_sum(mg * mg), row_sum(weighted * s), row_sum(weighted * mg)]
    mm, ss, smg, mgmg, ws, wmg = [v * (1.0 / d) for v in share_stats(at, wires, sums, stats, inbox)]
    inv_post = lax.rsqrt(mm + epsilon)
    inv_final = lax.rsqrt(ss + 2.0 * inv_post * smg + inv_post * inv_post * mgmg + epsilon)
    output = s + mg * inv_post
    lean = (inv_final * inv_final * inv_final) * (ws + inv_post * wmg)
    grad_output = inv_final * weighted - output * lean
    pull = inv_final * wmg - lean * (smg + inv_post * mgmg)
    grad_mlp = inv_post * (pg * grad_output) - m * (inv_post * inv_post * inv_post) * pull
    return grad_output, grad_mlp, ss


def last_grad(at, wires, total, stats, inbox, d, clean, pre_gain, grad_output, ss):
    width = total.shape[1]
    rows = rows16((at.mp * 2 + at.x) * 16)
    columns = pl.ds(pl.multiple_of(at.z * width, 128), width)
    s = clean[rows, columns].astype(F32)
    pre_grad = pre_gain[:, columns] * total[...]
    inv_pre = lax.rsqrt(ss + epsilon)
    (ps,) = share_stats(at, wires, [row_sum(pre_grad * s)], stats, inbox)
    return grad_output + inv_pre * pre_grad - s * (inv_pre * inv_pre * inv_pre) * (ps * (1.0 / d))


def first_kernel(depth, own, buf, send, recv):
    at = Place(depth)
    at.greet()
    run(gather_blocks(at, Wires(send, recv), own, buf))


def middle_kernel(depth, d, part, clean, answers, unembed, post_gain, final_gain, grads, grad_output_ref, ss_ref, send, recv, total, stats, inbox, own, *bufs):
    at = Place(depth)
    at.greet()
    wires = Wires(send, recv)
    run(scatter_sum(at, wires, part, bufs, total))
    grad_output, grad_mlp, ss = middle(at, wires, total, stats, inbox, d, clean, answers, unembed, post_gain, final_gain)
    grad_output_ref[...] = grad_output
    own[...] = grad_mlp.astype(BF)
    ss_ref[...] = jnp.broadcast_to(ss, ss_ref.shape)
    run(gather_rows(at, wires, own, grads))


def last_kernel(depth, d, part, clean, pre_gain, grad_output, ss, grads, send, recv, total, stats, inbox, own, *bufs):
    at = Place(depth)
    at.greet()
    wires = Wires(send, recv)
    run(scatter_sum(at, wires, part, bufs, total))
    own[...] = last_grad(at, wires, total, stats, inbox, d, clean, pre_gain, grad_output[...], ss[:, 0:1]).astype(BF)
    run(gather_rows(at, wires, own, grads))


def call(kernel, number, outs, scratch, operands):
    vmem = pl.BlockSpec(memory_space=pltpu.VMEM)
    return pl.pallas_call(
        kernel,
        out_shape=[jax.ShapeDtypeStruct(*o) for o in outs],
        in_specs=[vmem] * len(operands),
        out_specs=[vmem] * len(outs),
        scratch_shapes=[pltpu.SemaphoreType.DMA((48,)), pltpu.SemaphoreType.DMA((48,))] + scratch,
        compiler_params=pltpu.CompilerParams(
            collective_id=number, has_side_effects=True, vmem_limit_bytes=48 * 1024 * 1024
        ),
    )(*operands)


def staged(
    depth,
    resid_clean,
    resid_corrupt,
    answer_ids,
    unembed,
    pre_gain,
    post_gain,
    final_gain,
    w_gate,
    w_up,
    w_down,
    w_enc,
    b_enc,
    w_dec,
):
    own_rows, d = resid_clean.shape
    width = d // depth
    total_rows = own_rows * depth * 8
    pieces = 16 // own_rows
    own = jnp.concatenate([resid_clean.reshape(16, width), resid_corrupt.reshape(16, width)], axis=1)
    (buf,) = call(functools.partial(first_kernel, depth), 0, [((total_rows * pieces, 2 * width), BF)], [], [own])
    both = buf.reshape(2, 2, 2, depth, own_rows, pieces, 2, width)
    both = both.transpose(6, 1, 0, 3, 2, 4, 5, 7).reshape(2 * total_rows, d)
    clean_all = both[:total_rows]
    stream = clean_all.astype(F32)
    inv_pre = lax.rsqrt(jnp.mean(stream * stream, axis=-1, keepdims=True) + epsilon)
    normed = (stream * inv_pre * pre_gain).astype(BF)
    gate_pre = jnp.dot(normed, w_gate, preferred_element_type=F32)
    up_proj = jnp.dot(normed, w_up, preferred_element_type=F32)
    activated = gelu_tanh(gate_pre)
    hidden = (activated * up_proj).astype(BF)
    part = jnp.dot(hidden, w_down, preferred_element_type=F32).astype(BF)
    scratch = [
        pltpu.VMEM((16, width), F32), pltpu.VMEM((16, 128), F32), pltpu.VMEM((depth - 1, 16, 128), F32),
        pltpu.VMEM((16, width), BF),
    ] + scatter_buffers(d, depth)
    grad_mlp, grad_output, ss = call(
        functools.partial(middle_kernel, depth, d), 1,
        [((total_rows, d), BF), ((16, width), F32), ((16, 128), F32)], scratch,
        [part, clean_all, answer_ids, unembed, post_gain[None], final_gain[None]],
    )
    grad_hidden = contract_last(grad_mlp, w_down)
    grad_gate = (grad_hidden * up_proj * gelu_slope(gate_pre)).astype(BF)
    grad_up = (grad_hidden * activated).astype(BF)
    part = (contract_last(grad_gate, w_gate) + contract_last(grad_up, w_up)).astype(BF)
    (grad_stream,) = call(
        functools.partial(last_kernel, depth, d), 2, [((total_rows, d), BF)], scratch,
        [part, clean_all, pre_gain[None], grad_output, ss],
    )
    code = jax.nn.relu(jnp.dot(both, w_enc, preferred_element_type=F32) + b_enc)
    change = code[:total_rows] - code[total_rows:]
    product = change * contract_last(grad_stream, w_dec)
    return jnp.sum(product.reshape(total_rows // SEQ, SEQ, product.shape[1]), axis=1)


def fits(mesh, rows, d):
    depth = mesh.shape["latent"] // 2
    return (
        mesh.shape["mp"] == 4 and depth >= 2 and rows == 128 and 16 * mesh.shape["latent"] * 4 == rows * depth
        and d % (128 * depth) == 0 and d % 256 == 0
    )


def solution(mesh):
    def chosen(resid_clean, *rest):
        rows = resid_clean.shape[0] * mesh.shape["mp"] * mesh.shape["latent"]
        if fits(mesh, rows, resid_clean.shape[1]):
            return staged(mesh.shape["latent"] // 2, resid_clean, *rest)
        return local(resid_clean, *rest)

    return jax.shard_map(
        chosen,
        mesh=mesh,
        in_specs=(
            P(("mp", "latent"), None),
            P(("mp", "latent"), None),
            P(),
            P(),
            P(),
            P(),
            P(),
            P(None, ("mp", "latent")),
            P(None, ("mp", "latent")),
            P(("mp", "latent"), None),
            P(None, ("mp", "latent")),
            P(("mp", "latent")),
            P(("mp", "latent"), None),
        ),
        out_specs=P(None, ("mp", "latent")),
        check_vma=False,
    )
```

```python
import functools

import jax
import jax.numpy as jnp
from jax import lax
from jax.experimental import pallas as pl
from jax.experimental.pallas import tpu as pltpu
from jax.sharding import PartitionSpec as P

SEQ = 128


epsilon = 1e-06
gelu_scale = 0.7978845608028654
gelu_cubic = 0.044715


def gelu_tanh(value):
    return 0.5 * value * (1.0 + jnp.tanh(gelu_scale * (value + gelu_cubic * value * value * value)))


def gelu_slope(value):
    inner = jnp.tanh(gelu_scale * (value + gelu_cubic * value * value * value))
    return 0.5 * (1.0 + inner) + 0.5 * value * (1.0 - inner * inner) * gelu_scale * (
        1.0 + 3.0 * gelu_cubic * value * value
    )


def contract_last(left, right):
    return lax.dot_general(
        left, right, (((1,), (1,)), ((), ())), preferred_element_type=jnp.float32
    )


def output_grads(stream, mlp_out, answers, unembed, post_gain, final_gain):
    inv_post = lax.rsqrt(jnp.mean(mlp_out * mlp_out, axis=-1, keepdims=True) + epsilon)
    output = stream + mlp_out * inv_post * post_gain
    inv_final = lax.rsqrt(jnp.mean(output * output, axis=-1, keepdims=True) + epsilon)
    candidate = lax.broadcasted_iota(jnp.int32, (answers.shape[0], unembed.shape[0]), 1)
    selector = (
        (candidate == answers[:, 0:1]).astype(jnp.float32)
        - (candidate == answers[:, 1:2]).astype(jnp.float32)
    ).astype(jnp.bfloat16)
    direction = jnp.dot(selector, unembed, preferred_element_type=jnp.float32)
    weighted = final_gain * direction
    grad_output = inv_final * weighted - output * (inv_final * inv_final * inv_final) * jnp.mean(
        weighted * output, axis=-1, keepdims=True
    )
    post_grad = post_gain * grad_output
    grad_mlp = (
        inv_post * post_grad
        - mlp_out
        * (inv_post * inv_post * inv_post)
        * jnp.mean(post_grad * mlp_out, axis=-1, keepdims=True)
    ).astype(jnp.bfloat16)
    return (grad_output, grad_mlp)


def local(
    resid_clean,
    resid_corrupt,
    answer_ids,
    unembed,
    pre_gain,
    post_gain,
    final_gain,
    w_gate,
    w_up,
    w_down,
    w_enc,
    b_enc,
    w_dec,
):
    own_rows = resid_clean.shape[0]
    clean_all, corrupt_all = (
        lax.all_gather(resid_clean, ("mp", "latent"), axis=0, tiled=True),
        lax.all_gather(resid_corrupt, ("mp", "latent"), axis=0, tiled=True),
    )
    total_rows = clean_all.shape[0]
    offset = lax.axis_index(("mp", "latent")) * own_rows
    stream = clean_all.astype(jnp.float32)
    inv_pre = lax.rsqrt(jnp.mean(stream * stream, axis=-1, keepdims=True) + epsilon)
    normed = (stream * inv_pre * pre_gain).astype(jnp.bfloat16)
    gate_pre = jnp.dot(normed, w_gate, preferred_element_type=jnp.float32)
    up_proj = jnp.dot(normed, w_up, preferred_element_type=jnp.float32)
    activated = gelu_tanh(gate_pre)
    hidden = (activated * up_proj).astype(jnp.bfloat16)
    stream_rows = lax.dynamic_slice_in_dim(stream, offset, own_rows, 0)
    inv_rows = lax.dynamic_slice_in_dim(inv_pre, offset, own_rows, 0)
    mlp_out = lax.psum(
        jnp.dot(hidden, w_down, preferred_element_type=jnp.float32), ("mp", "latent")
    )
    grad_output, grad_mlp = output_grads(
        stream, mlp_out, answer_ids, unembed, post_gain, final_gain
    )
    grad_hidden = contract_last(grad_mlp, w_down)
    grad_rows_out = lax.dynamic_slice_in_dim(grad_output, offset, own_rows, 0)
    grad_gate = (grad_hidden * up_proj * gelu_slope(gate_pre)).astype(jnp.bfloat16)
    grad_up = (grad_hidden * activated).astype(jnp.bfloat16)
    grad_normed = lax.psum_scatter(
        contract_last(grad_gate, w_gate) + contract_last(grad_up, w_up),
        ("mp", "latent"),
        scatter_dimension=0,
        tiled=True,
    )
    pre_grad = pre_gain * grad_normed
    grad_stream = (
        grad_rows_out
        + inv_rows * pre_grad
        - stream_rows
        * (inv_rows * inv_rows * inv_rows)
        * jnp.mean(pre_grad * stream_rows, axis=-1, keepdims=True)
    ).astype(jnp.bfloat16)
    clean_code = jax.nn.relu(jnp.dot(clean_all, w_enc, preferred_element_type=jnp.float32) + b_enc)
    corrupt_code = jax.nn.relu(
        jnp.dot(corrupt_all, w_enc, preferred_element_type=jnp.float32) + b_enc
    )
    change = clean_code - corrupt_code
    projected = contract_last(
        lax.all_gather(grad_stream, ("mp", "latent"), axis=0, tiled=True), w_dec
    )
    product = change * projected
    return jnp.sum(product.reshape(total_rows // SEQ, SEQ, product.shape[1]), axis=1)


MESH = pl.DeviceIdType.MESH
BF = jnp.bfloat16
F32 = jnp.float32


class Place:
    def __init__(self, depth):
        self.depth = depth
        self.mp = lax.axis_index("mp")
        self.lat = lax.axis_index("latent")
        self.c, self.y = self.mp % 2, self.mp // 2
        self.x, self.z = self.lat % 2, self.lat // 2
        self.core_peer = (self.y * 2 + 1 - self.c, self.lat)
        self.mp_y = (1 - self.y) * 2 + self.c
        self.y_peer = (self.mp_y, self.lat)
        self.x_peer = (self.mp, self.z * 2 + 1 - self.x)

    def z_peer(self, step):
        return (self.mp, ((self.z + step) % self.depth) * 2 + self.x)

    def greet(self):
        barrier = pltpu.get_barrier_semaphore()
        peers = [self.core_peer, self.y_peer, self.x_peer]
        peers += [self.z_peer(step) for step in range(1, self.depth)]
        for peer in peers:
            pl.semaphore_signal(barrier, inc=1, device_id=peer, device_id_type=MESH)
        pl.semaphore_wait(barrier, len(peers))


class Wires:
    def __init__(self, send, recv):
        self.send, self.recv, self.used = send, recv, 0

    def start(self, src, dst, peer):
        i = self.used
        self.used += 1
        copy = pltpu.make_async_remote_copy(
            src_ref=src, dst_ref=dst, send_sem=self.send.at[i], recv_sem=self.recv.at[i],
            device_id=peer, device_id_type=MESH,
        )
        copy.start()
        return copy


def finish(copies):
    for copy in copies:
        copy.wait()


def rows16(start):
    return pl.ds(pl.multiple_of(start, 16), 16)


def rows32(start):
    return pl.ds(pl.multiple_of(start, 32), 32)


def gather_blocks(at, wires, own, buf):
    depth = at.depth
    cut = (buf.shape[1] // 256) * 128
    half0, half1 = pl.ds(0, cut), pl.ds(cut, buf.shape[1] - cut)
    lane = ((at.c * 2 + at.y) * 2 + at.x) * depth
    quad = depth * 16
    mine = rows16((lane + at.z) * 16)
    group = pl.ds(pl.multiple_of(lane * 16, quad), quad)
    group_y = pl.ds(pl.multiple_of(((at.c * 2 + 1 - at.y) * 2 + at.x) * quad, quad), quad)
    pair = pl.ds(pl.multiple_of((at.c * 2 + at.y) * 2 * quad, quad), 2 * quad)
    side = pl.ds(pl.multiple_of(at.c * 4 * quad, quad), 4 * quad)
    first = [wires.start(own, buf.at[mine], at.z_peer(s)) for s in range(1, depth)]
    buf[mine, :] = own[...]
    yield
    finish(first)
    cx = wires.start(buf.at[group, half0], buf.at[group, half0], at.x_peer)
    cy = wires.start(buf.at[group, half1], buf.at[group, half1], at.y_peer)
    yield
    finish([cx, cy])
    cy = wires.start(buf.at[pair, half0], buf.at[pair, half0], at.y_peer)
    cx = wires.start(buf.at[group, half1], buf.at[group, half1], at.x_peer)
    cx2 = wires.start(buf.at[group_y, half1], buf.at[group_y, half1], at.x_peer)
    yield
    finish([cy, cx, cx2])
    core = wires.start(buf.at[side], buf.at[side], at.core_peer)
    yield
    finish([core])


def gather_rows(at, wires, own, buf):
    depth = at.depth
    width = own.shape[1]
    half = buf.shape[1] // 2
    halves = (pl.ds(0, half), pl.ds(half, half))
    mine = rows16((at.mp * 2 + at.x) * 16)
    other = rows16((at.mp_y * 2 + at.x) * 16)
    both = rows32(at.mp * 32)
    both_y = rows32(at.mp_y * 32)
    spot = buf.at[mine, pl.ds(pl.multiple_of(at.z * width, 128), width)]
    first = [wires.start(own, spot, at.z_peer(s)) for s in range(1, depth)]
    buf[mine, pl.ds(pl.multiple_of(at.z * width, 128), width)] = own[...]
    yield
    finish(first)

    def share(rows, h, peer):
        spot = buf.at[rows, halves[h]]
        return wires.start(spot, spot, peer)

    step = [share(mine, 0, at.x_peer), share(mine, 1, at.y_peer)]
    yield
    finish(step)
    core = [share(both, 0, at.core_peer)]
    step = [share(both, 0, at.y_peer), share(mine, 1, at.x_peer), share(other, 1, at.x_peer)]
    yield
    finish(step)
    core += [share(both_y, 0, at.core_peer), share(both, 1, at.core_peer), share(both_y, 1, at.core_peer)]
    yield
    finish(core)


def scatter_sum(at, wires, part, bufs, total, produce):
    rc, s1, ry, s2a, rx, s2b, rx2, ry2, s3, rz = bufs
    depth = at.depth
    width = total.shape[1]
    half = part.shape[1] // 2
    h0, h1 = pl.ds(0, half), pl.ds(half, half)
    core = []
    for i, h in enumerate((h0, h1)):
        produce(i)
        for yy in range(2):
            core.append(wires.start(
                part.at[rows32((yy * 2 + 1 - at.c) * 32), h], rc.at[yy, :, h], at.core_peer))
    own16, peer16 = rows16(at.x * 16), rows16((1 - at.x) * 16)
    yield
    finish(core[:2])
    for yy in range(2):
        s1[yy, :, h0] = (part[rows32((yy * 2 + at.c) * 32), h0].astype(F32) + rc[yy, :, h0].astype(F32)).astype(BF)
    cy = wires.start(s1.at[1 - at.y, :, h0], ry, at.y_peer)
    finish(core[2:])
    for yy in range(2):
        s1[yy, :, h1] = (part[rows32((yy * 2 + at.c) * 32), h1].astype(F32) + rc[yy, :, h1].astype(F32)).astype(BF)
    cx = [wires.start(s1.at[yy, peer16, h1], rx.at[yy], at.x_peer) for yy in range(2)]
    yield
    finish([cy])
    s2a[...] = (s1[at.y, :, h0].astype(F32) + ry[...].astype(F32)).astype(BF)
    cx2 = wires.start(s2a.at[peer16], rx2, at.x_peer)
    finish(cx)
    for yy in range(2):
        s2b[yy] = (s1[yy, own16, h1].astype(F32) + rx[yy].astype(F32)).astype(BF)
    cy2 = wires.start(s2b.at[1 - at.y], ry2, at.y_peer)
    yield
    finish([cx2])
    s3[:, h0] = (s2a[own16, :].astype(F32) + rx2[...].astype(F32)).astype(BF)
    finish([cy2])
    s3[:, h1] = (s2b[at.y].astype(F32) + ry2[...].astype(F32)).astype(BF)
    last = []
    for s in range(1, depth):
        column = pl.multiple_of(((at.z + s) % depth) * width, 128)
        last.append(wires.start(s3.at[:, pl.ds(column, width)], rz.at[s - 1], at.z_peer(s)))
    yield
    finish(last)
    value = s3[:, pl.ds(pl.multiple_of(at.z * width, 128), width)].astype(F32)
    for s in range(1, depth):
        value = value + rz[s - 1].astype(F32)
    total[...] = value


def scatter_buffers(d, depth):
    half, width = d // 2, d // depth
    return [
        pltpu.VMEM((2, 32, d), BF), pltpu.VMEM((2, 32, d), BF), pltpu.VMEM((32, half), BF),
        pltpu.VMEM((32, half), BF), pltpu.VMEM((2, 16, half), BF), pltpu.VMEM((2, 16, half), BF),
        pltpu.VMEM((16, half), BF), pltpu.VMEM((16, half), BF), pltpu.VMEM((16, d), BF),
        pltpu.VMEM((depth - 1, 16, width), BF),
    ]


def share_stats(at, wires, sums, out, inbox):
    lane = lax.broadcasted_iota(jnp.int32, (16, 128), 1)
    packed = jnp.zeros((16, 128), F32)
    for i, value in enumerate(sums):
        packed = jnp.where(lane == i, value, packed)
    out[...] = packed
    finish([wires.start(out, inbox.at[s - 1], at.z_peer(s)) for s in range(1, at.depth)])
    for s in range(1, at.depth):
        packed = packed + inbox[s - 1]
    return [packed[:, i : i + 1] for i in range(len(sums))]


def row_sum(value):
    return jnp.sum(value, axis=-1, keepdims=True)


def run(steps, work=()):
    work = iter(work)
    for _ in steps:
        next(work, None)


def middle(at, wires, total, stats, inbox, d, clean, answers, unembed, post_gain, final_gain):
    width = total.shape[1]
    rows = rows16((at.mp * 2 + at.x) * 16)
    columns = pl.ds(pl.multiple_of(at.z * width, 128), width)
    m = total[...]
    s = clean[rows, columns].astype(F32)
    pg = post_gain[:, columns]
    ids = answers[rows, :]
    candidate = lax.broadcasted_iota(jnp.int32, (16, unembed.shape[0]), 1)
    selector = (
        jnp.where(candidate == ids[:, 0:1], 1.0, 0.0) - jnp.where(candidate == ids[:, 1:2], 1.0, 0.0)
    ).astype(BF)
    direction = jnp.dot(selector, unembed[:, columns], preferred_element_type=F32)
    weighted = final_gain[:, columns] * direction
    mg = m * pg
    sums = [row_sum(m * m), row_sum(s * s), row_sum(s * mg), row_sum(mg * mg), row_sum(weighted * s), row_sum(weighted * mg)]
    mm, ss, smg, mgmg, ws, wmg = [v * (1.0 / d) for v in share_stats(at, wires, sums, stats, inbox)]
    inv_post = lax.rsqrt(mm + epsilon)
    inv_final = lax.rsqrt(ss + 2.0 * inv_post * smg + inv_post * inv_post * mgmg + epsilon)
    output = s + mg * inv_post
    lean = (inv_final * inv_final * inv_final) * (ws + inv_post * wmg)
    grad_output = inv_final * weighted - output * lean
    pull = inv_final * wmg - lean * (smg + inv_post * mgmg)
    grad_mlp = inv_post * (pg * grad_output) - m * (inv_post * inv_post * inv_post) * pull
    return grad_output, grad_mlp, ss


def last_grad(at, wires, total, stats, inbox, d, clean, pre_gain, grad_output, ss):
    width = total.shape[1]
    rows = rows16((at.mp * 2 + at.x) * 16)
    columns = pl.ds(pl.multiple_of(at.z * width, 128), width)
    s = clean[rows, columns].astype(F32)
    pre_grad = pre_gain[:, columns] * total[...]
    inv_pre = lax.rsqrt(ss + epsilon)
    (ps,) = share_stats(at, wires, [row_sum(pre_grad * s)], stats, inbox)
    return grad_output + inv_pre * pre_grad - s * (inv_pre * inv_pre * inv_pre) * (ps * (1.0 / d))


def whole_kernel(
    depth, pieces, own_clean, own_corrupt, target, answers, gains, b_enc, unembed_hbm, wg_hbm, wu_hbm, wd_hbm, we_hbm, wl_hbm, out,
    send, recv, load, wg, wu, wd, we, wl, unembed, buf0, buf1, xs, normed, gate_pre, up, hidden, grad_gate, grad_up,
    part, grads, change, kept, total, stats, inbox, own, *bufs,
):
    d, units = wg.shape
    latents = out.shape[1]
    rows = normed.shape[0]
    width = d // depth
    tile = we.shape[2]
    first = latents // 2
    pre_gain, post_gain, final_gain = gains.at[0:1], gains.at[1:2], gains.at[2:3]
    loads = [
        pltpu.make_async_copy(wg_hbm, wg, load.at[0]),
        pltpu.make_async_copy(wu_hbm, wu, load.at[1]),
        pltpu.make_async_copy(wd_hbm, wd, load.at[2]),
        pltpu.make_async_copy(unembed_hbm, unembed, load.at[3]),
        pltpu.make_async_copy(wl_hbm.at[first:latents], wl, load.at[4]),
    ]
    low = pltpu.make_async_copy(wl_hbm.at[0:first], wd.at[0:first], load.at[5])
    count = latents // tile

    def piece(p):
        return pltpu.make_async_copy(we_hbm.at[:, p * tile : (p + 1) * tile], we.at[p % 2], load.at[6 + p % 2])

    for copy in loads[:4]:
        copy.start()
    at = Place(depth)
    at.greet()
    wires = Wires(send, recv)
    run(gather_blocks(at, wires, own_clean, buf0))
    piece(0).start()
    piece(1).start()
    loads[4].start()
    side = gather_blocks(at, wires, own_corrupt, buf1)
    next(side, None)

    def arrange(buf, base):
        place = lax.broadcasted_iota(jnp.int32, (rows, rows * pieces), 1)
        for s in range(depth):
            pick = jnp.where(place == target[...] + s, 1.0, 0.0).astype(BF)
            xs[base : base + rows, s * width : (s + 1) * width] = jnp.dot(pick, buf[...], preferred_element_type=F32).astype(BF)

    arrange(buf0, 0)

    @pl.loop(0, rows // 16)
    def _(i):
        span = rows16(i * 16)
        stream = xs[span, :].astype(F32)
        inv_pre = lax.rsqrt(row_sum(stream * stream) * (1.0 / d) + epsilon)
        normed[span, :] = (stream * inv_pre * pre_gain[...]).astype(BF)

    next(side, None)
    loads[0].wait()
    loads[1].wait()
    cuts = [(a, min(a + 256, units)) for a in range(0, units, 256)]
    for n, (a, b) in enumerate(cuts):
        gate = jnp.dot(normed[...], wg[:, a:b], preferred_element_type=F32)
        lift = jnp.dot(normed[...], wu[:, a:b], preferred_element_type=F32)
        gate_pre[:, a:b] = gate
        up[:, a:b] = lift
        hidden[:, a:b] = (gelu_tanh(gate) * lift).astype(BF)
        if n % 2 == 1:
            next(side, None)
    for _ in side:
        pass
    loads[2].wait()
    half = d // 2

    def forward(h):
        @pl.loop(0, half // 256)
        def _(i):
            span = pl.ds(pl.multiple_of(h * half + i * 256, 256), 256)
            part[:, span] = jnp.dot(hidden[...], wd[:, span], preferred_element_type=F32).astype(BF)

    def encode():
        for p in range(count):
            if p == 0:
                arrange(buf1, rows)
            piece(p).wait()
            span = slice(p * tile, (p + 1) * tile)
            code = jnp.dot(xs[...], we[p % 2], preferred_element_type=F32) + b_enc[:, span]
            code = jnp.maximum(code, 0.0)
            change[:, span] = code[:rows] - code[rows:]
            if p + 2 < count:
                piece(p + 2).start()
            yield

    clean = xs.at[0:rows]
    work = encode()
    run(scatter_sum(at, wires, part, bufs, total, forward), work)
    loads[3].wait()
    grad_output, grad_mlp, ss = middle(
        at, wires, total, stats, inbox, d, clean, answers, unembed, post_gain, final_gain
    )
    kept[...] = grad_output
    own[...] = grad_mlp.astype(BF)
    run(gather_rows(at, wires, own, grads), work)
    for a, b in cuts:
        grad_hidden = contract_last(grads[...], wd[a:b, :])
        gate = gate_pre[:, a:b]
        grad_gate[:, a:b] = (grad_hidden * up[:, a:b] * gelu_slope(gate)).astype(BF)
        grad_up[:, a:b] = (grad_hidden * gelu_tanh(gate)).astype(BF)
    low.start()

    def backward(h):
        @pl.loop(0, half // 256)
        def _(i):
            span = pl.ds(pl.multiple_of(h * half + i * 256, 256), 256)
            value = contract_last(grad_gate[...], wg[span, :]) + contract_last(grad_up[...], wu[span, :])
            part[:, span] = value.astype(BF)

    run(scatter_sum(at, wires, part, bufs, total, backward), work)
    own[...] = last_grad(at, wires, total, stats, inbox, d, clean, pre_gain, kept[...], ss).astype(BF)
    run(gather_rows(at, wires, own, grads), work)
    for _ in work:
        pass
    low.wait()
    loads[4].wait()
    for p in range(count):
        source = wd if (p + 1) * tile <= first else wl
        base = p * tile % first
        projected = contract_last(grads[...], source[base : base + tile, :])
        span = slice(p * tile, (p + 1) * tile)
        out[:, span] = jnp.sum(change[:, span] * projected, axis=0, keepdims=True)


def staged(
    depth,
    resid_clean,
    resid_corrupt,
    answer_ids,
    unembed,
    pre_gain,
    post_gain,
    final_gain,
    w_gate,
    w_up,
    w_down,
    w_enc,
    b_enc,
    w_dec,
):
    own_rows, d = resid_clean.shape
    width = d // depth
    units = w_gate.shape[1]
    latents = w_enc.shape[1]
    rows = own_rows * depth * 8
    pieces = 16 // own_rows
    tile = 256
    token = jnp.arange(rows, dtype=jnp.int32)[:, None]
    device = token // own_rows
    x, z = device % 2, device // 2 % depth
    c, y = device // (2 * depth) % 2, device // (4 * depth)
    target = (((c * 2 + y) * 2 + x) * depth + z) * 16 + token % own_rows * pieces
    vmem = pl.BlockSpec(memory_space=pltpu.VMEM)
    hbm = pl.BlockSpec(memory_space=pl.ANY)
    scratch = [
        pltpu.SemaphoreType.DMA((80,)), pltpu.SemaphoreType.DMA((80,)), pltpu.SemaphoreType.DMA((8,)),
        pltpu.VMEM((d, units), BF), pltpu.VMEM((d, units), BF), pltpu.VMEM((units, d), BF),
        pltpu.VMEM((2, d, tile), BF), pltpu.VMEM((latents // 2, d), BF), pltpu.VMEM(unembed.shape, BF),
        pltpu.VMEM((rows * pieces, width), BF), pltpu.VMEM((rows * pieces, width), BF),
        pltpu.VMEM((2 * rows, d), BF), pltpu.VMEM((rows, d), BF),
        pltpu.VMEM((rows, units), F32), pltpu.VMEM((rows, units), F32), pltpu.VMEM((rows, units), BF),
        pltpu.VMEM((rows, units), BF), pltpu.VMEM((rows, units), BF),
        pltpu.VMEM((rows, d), BF), pltpu.VMEM((rows, d), BF), pltpu.VMEM((rows, latents), F32),
        pltpu.VMEM((16, width), F32), pltpu.VMEM((16, width), F32), pltpu.VMEM((16, 128), F32),
        pltpu.VMEM((depth - 1, 16, 128), F32), pltpu.VMEM((16, width), BF),
    ] + scatter_buffers(d, depth)
    return pl.pallas_call(
        functools.partial(whole_kernel, depth, pieces),
        out_shape=jax.ShapeDtypeStruct((1, latents), F32),
        in_specs=[vmem] * 6 + [hbm] * 6,
        out_specs=vmem,
        scratch_shapes=scratch,
        compiler_params=pltpu.CompilerParams(
            collective_id=0, has_side_effects=True, vmem_limit_bytes=67043328
        ),
    )(
        resid_clean.reshape(16, width), resid_corrupt.reshape(16, width), target, answer_ids,
        jnp.stack([pre_gain, post_gain, final_gain]), b_enc[None], unembed, w_gate, w_up, w_down, w_enc, w_dec,
    )


def fits(mesh, rows, d, units, latents):
    depth = mesh.shape["latent"] // 2
    return (
        mesh.shape["mp"] == 4 and depth >= 2 and rows == 128 and 16 * mesh.shape["latent"] * 4 == rows * depth
        and d % (128 * depth) == 0 and d % 512 == 0
        and rows == SEQ and units % 128 == 0 and latents % 512 == 0 and latents // 2 <= units
    )


def solution(mesh):
    def chosen(resid_clean, *rest):
        rows = resid_clean.shape[0] * mesh.shape["mp"] * mesh.shape["latent"]
        if fits(mesh, rows, resid_clean.shape[1], rest[6].shape[1], rest[9].shape[1]):
            return staged(mesh.shape["latent"] // 2, resid_clean, *rest)
        return local(resid_clean, *rest)

    return jax.shard_map(
        chosen,
        mesh=mesh,
        in_specs=(
            P(("mp", "latent"), None),
            P(("mp", "latent"), None),
            P(),
            P(),
            P(),
            P(),
            P(),
            P(None, ("mp", "latent")),
            P(None, ("mp", "latent")),
            P(("mp", "latent"), None),
            P(None, ("mp", "latent")),
            P(("mp", "latent")),
            P(("mp", "latent"), None),
        ),
        out_specs=P(None, ("mp", "latent")),
        check_vma=False,
    )
```

```python
import functools

import jax
import jax.numpy as jnp
import numpy as np
from jax import lax
from jax.experimental import pallas as pl
from jax.experimental.pallas import tpu as pltpu
from jax.sharding import PartitionSpec as P

SEQ = 128


epsilon = 1e-06
gelu_scale = 0.7978845608028654
gelu_cubic = 0.044715


def gelu_tanh(value):
    return 0.5 * value * (1.0 + jnp.tanh(gelu_scale * (value + gelu_cubic * value * value * value)))


def gelu_slope(value):
    inner = jnp.tanh(gelu_scale * (value + gelu_cubic * value * value * value))
    return 0.5 * (1.0 + inner) + 0.5 * value * (1.0 - inner * inner) * gelu_scale * (
        1.0 + 3.0 * gelu_cubic * value * value
    )


def contract_last(left, right):
    return lax.dot_general(
        left, right, (((1,), (1,)), ((), ())), preferred_element_type=jnp.float32
    )


def output_grads(stream, mlp_out, answers, unembed, post_gain, final_gain):
    inv_post = lax.rsqrt(jnp.mean(mlp_out * mlp_out, axis=-1, keepdims=True) + epsilon)
    output = stream + mlp_out * inv_post * post_gain
    inv_final = lax.rsqrt(jnp.mean(output * output, axis=-1, keepdims=True) + epsilon)
    candidate = lax.broadcasted_iota(jnp.int32, (answers.shape[0], unembed.shape[0]), 1)
    selector = (
        (candidate == answers[:, 0:1]).astype(jnp.float32)
        - (candidate == answers[:, 1:2]).astype(jnp.float32)
    ).astype(jnp.bfloat16)
    direction = jnp.dot(selector, unembed, preferred_element_type=jnp.float32)
    weighted = final_gain * direction
    grad_output = inv_final * weighted - output * (inv_final * inv_final * inv_final) * jnp.mean(
        weighted * output, axis=-1, keepdims=True
    )
    post_grad = post_gain * grad_output
    grad_mlp = (
        inv_post * post_grad
        - mlp_out
        * (inv_post * inv_post * inv_post)
        * jnp.mean(post_grad * mlp_out, axis=-1, keepdims=True)
    ).astype(jnp.bfloat16)
    return (grad_output, grad_mlp)


def local(
    resid_clean,
    resid_corrupt,
    answer_ids,
    unembed,
    pre_gain,
    post_gain,
    final_gain,
    w_gate,
    w_up,
    w_down,
    w_enc,
    b_enc,
    w_dec,
):
    own_rows = resid_clean.shape[0]
    clean_all, corrupt_all = (
        lax.all_gather(resid_clean, ("mp", "latent"), axis=0, tiled=True),
        lax.all_gather(resid_corrupt, ("mp", "latent"), axis=0, tiled=True),
    )
    total_rows = clean_all.shape[0]
    offset = lax.axis_index(("mp", "latent")) * own_rows
    stream = clean_all.astype(jnp.float32)
    inv_pre = lax.rsqrt(jnp.mean(stream * stream, axis=-1, keepdims=True) + epsilon)
    normed = (stream * inv_pre * pre_gain).astype(jnp.bfloat16)
    gate_pre = jnp.dot(normed, w_gate, preferred_element_type=jnp.float32)
    up_proj = jnp.dot(normed, w_up, preferred_element_type=jnp.float32)
    activated = gelu_tanh(gate_pre)
    hidden = (activated * up_proj).astype(jnp.bfloat16)
    stream_rows = lax.dynamic_slice_in_dim(stream, offset, own_rows, 0)
    inv_rows = lax.dynamic_slice_in_dim(inv_pre, offset, own_rows, 0)
    mlp_out = lax.psum(
        jnp.dot(hidden, w_down, preferred_element_type=jnp.float32), ("mp", "latent")
    )
    grad_output, grad_mlp = output_grads(
        stream, mlp_out, answer_ids, unembed, post_gain, final_gain
    )
    grad_hidden = contract_last(grad_mlp, w_down)
    grad_rows_out = lax.dynamic_slice_in_dim(grad_output, offset, own_rows, 0)
    grad_gate = (grad_hidden * up_proj * gelu_slope(gate_pre)).astype(jnp.bfloat16)
    grad_up = (grad_hidden * activated).astype(jnp.bfloat16)
    grad_normed = lax.psum_scatter(
        contract_last(grad_gate, w_gate) + contract_last(grad_up, w_up),
        ("mp", "latent"),
        scatter_dimension=0,
        tiled=True,
    )
    pre_grad = pre_gain * grad_normed
    grad_stream = (
        grad_rows_out
        + inv_rows * pre_grad
        - stream_rows
        * (inv_rows * inv_rows * inv_rows)
        * jnp.mean(pre_grad * stream_rows, axis=-1, keepdims=True)
    ).astype(jnp.bfloat16)
    clean_code = jax.nn.relu(jnp.dot(clean_all, w_enc, preferred_element_type=jnp.float32) + b_enc)
    corrupt_code = jax.nn.relu(
        jnp.dot(corrupt_all, w_enc, preferred_element_type=jnp.float32) + b_enc
    )
    change = clean_code - corrupt_code
    projected = contract_last(
        lax.all_gather(grad_stream, ("mp", "latent"), axis=0, tiled=True), w_dec
    )
    product = change * projected
    return jnp.sum(product.reshape(total_rows // SEQ, SEQ, product.shape[1]), axis=1)


MESH = pl.DeviceIdType.MESH
BF = jnp.bfloat16
F32 = jnp.float32


class Place:
    def __init__(self, depth):
        self.depth = depth
        self.mp = lax.axis_index("mp")
        self.lat = lax.axis_index("latent")
        self.c, self.y = self.mp % 2, self.mp // 2
        self.x, self.z = self.lat % 2, self.lat // 2
        self.core_peer = (self.y * 2 + 1 - self.c, self.lat)
        self.mp_y = (1 - self.y) * 2 + self.c
        self.y_peer = (self.mp_y, self.lat)
        self.x_peer = (self.mp, self.z * 2 + 1 - self.x)

    def z_peer(self, step):
        return (self.mp, ((self.z + step) % self.depth) * 2 + self.x)

    def greet(self):
        barrier = pltpu.get_barrier_semaphore()
        peers = [self.core_peer, self.y_peer, self.x_peer]
        peers += [self.z_peer(step) for step in range(1, self.depth)]
        for peer in peers:
            pl.semaphore_signal(barrier, inc=1, device_id=peer, device_id_type=MESH)
        pl.semaphore_wait(barrier, len(peers))


class Wires:
    def __init__(self, send, recv):
        self.send, self.recv, self.used = send, recv, 0

    def start(self, src, dst, peer):
        i = self.used
        self.used += 1
        copy = pltpu.make_async_remote_copy(
            src_ref=src, dst_ref=dst, send_sem=self.send.at[i], recv_sem=self.recv.at[i],
            device_id=peer, device_id_type=MESH,
        )
        copy.start()
        return copy


def finish(copies):
    for copy in copies:
        copy.wait()


def rows16(start):
    return pl.ds(pl.multiple_of(start, 16), 16)


def rows32(start):
    return pl.ds(pl.multiple_of(start, 32), 32)


def gather_blocks(at, wires, own, buf):
    depth = at.depth
    cut = (buf.shape[1] // 256) * 128
    half0, half1 = pl.ds(0, cut), pl.ds(cut, buf.shape[1] - cut)
    lane = ((at.c * 2 + at.y) * 2 + at.x) * depth
    quad = depth * 16
    mine = rows16((lane + at.z) * 16)
    group = pl.ds(pl.multiple_of(lane * 16, quad), quad)
    group_y = pl.ds(pl.multiple_of(((at.c * 2 + 1 - at.y) * 2 + at.x) * quad, quad), quad)
    pair = pl.ds(pl.multiple_of((at.c * 2 + at.y) * 2 * quad, quad), 2 * quad)
    side = pl.ds(pl.multiple_of(at.c * 4 * quad, quad), 4 * quad)
    first = [wires.start(own, buf.at[mine], at.z_peer(s)) for s in range(1, depth)]
    buf[mine, :] = own[...]
    yield
    finish(first)
    cx = wires.start(buf.at[group, half0], buf.at[group, half0], at.x_peer)
    cy = wires.start(buf.at[group, half1], buf.at[group, half1], at.y_peer)
    yield
    finish([cx, cy])
    cy = wires.start(buf.at[pair, half0], buf.at[pair, half0], at.y_peer)
    cx = wires.start(buf.at[group, half1], buf.at[group, half1], at.x_peer)
    cx2 = wires.start(buf.at[group_y, half1], buf.at[group_y, half1], at.x_peer)
    yield
    finish([cy, cx, cx2])
    core = wires.start(buf.at[side], buf.at[side], at.core_peer)
    yield
    finish([core])


def gather_rows(at, wires, own, buf):
    depth = at.depth
    width = own.shape[1]
    half = buf.shape[1] // 2
    halves = (pl.ds(0, half), pl.ds(half, half))
    mine = rows16((at.mp * 2 + at.x) * 16)
    other = rows16((at.mp_y * 2 + at.x) * 16)
    both = rows32(at.mp * 32)
    both_y = rows32(at.mp_y * 32)
    spot = buf.at[mine, pl.ds(pl.multiple_of(at.z * width, 128), width)]
    first = [wires.start(own, spot, at.z_peer(s)) for s in range(1, depth)]
    buf[mine, pl.ds(pl.multiple_of(at.z * width, 128), width)] = own[...]
    yield
    finish(first)

    def share(rows, h, peer):
        spot = buf.at[rows, halves[h]]
        return wires.start(spot, spot, peer)

    step = [share(mine, 0, at.x_peer), share(mine, 1, at.y_peer)]
    core = [share(mine, 0, at.core_peer), share(mine, 1, at.core_peer)]
    yield
    finish(step)
    near = rows16((at.mp * 2 + 1 - at.x) * 16)
    far = rows16((at.mp_y * 2 + 1 - at.x) * 16)
    step = [share(both, 0, at.y_peer), share(mine, 1, at.x_peer), share(other, 1, at.x_peer)]
    core += [share(near, 0, at.core_peer), share(other, 1, at.core_peer)]
    yield
    finish(step)
    core += [share(both_y, 0, at.core_peer), share(near, 1, at.core_peer), share(far, 1, at.core_peer)]
    yield
    finish(core)


def scatter_sum(at, wires, part, bufs, total, produce):
    rc, s1, ry, s2a, rx, s2b, rx2, ry2, s3, rz = bufs
    depth = at.depth
    width = total.shape[1]
    half = part.shape[1] // 2
    h0, h1 = pl.ds(0, half), pl.ds(half, half)
    own16, peer16 = rows16(at.x * 16), rows16((1 - at.x) * 16)

    def swap(h):
        return [
            wires.start(part.at[rows32((yy * 2 + 1 - at.c) * 32), h], rc.at[yy, :, h], at.core_peer)
            for yy in range(2)
        ]

    def merge(h):
        for yy in range(2):
            s1[yy, :, h] = (part[rows32((yy * 2 + at.c) * 32), h].astype(F32) + rc[yy, :, h].astype(F32)).astype(BF)

    produce(0, 2)
    core0 = swap(h0)
    produce(2, 3)
    finish(core0)
    merge(h0)
    cy = wires.start(s1.at[1 - at.y, :, h0], ry, at.y_peer)
    produce(3, 4)
    core1 = swap(h1)
    yield
    finish(core1)
    merge(h1)
    cx = [wires.start(s1.at[yy, peer16, h1], rx.at[yy], at.x_peer) for yy in range(2)]
    yield
    finish([cy])
    s2a[...] = (s1[at.y, :, h0].astype(F32) + ry[...].astype(F32)).astype(BF)
    cx2 = wires.start(s2a.at[peer16], rx2, at.x_peer)
    finish(cx)
    for yy in range(2):
        s2b[yy] = (s1[yy, own16, h1].astype(F32) + rx[yy].astype(F32)).astype(BF)
    cy2 = wires.start(s2b.at[1 - at.y], ry2, at.y_peer)
    yield
    finish([cx2])
    s3[:, h0] = (s2a[own16, :].astype(F32) + rx2[...].astype(F32)).astype(BF)
    finish([cy2])
    s3[:, h1] = (s2b[at.y].astype(F32) + ry2[...].astype(F32)).astype(BF)
    last = []
    for s in range(1, depth):
        column = pl.multiple_of(((at.z + s) % depth) * width, 128)
        last.append(wires.start(s3.at[:, pl.ds(column, width)], rz.at[s - 1], at.z_peer(s)))
    yield
    finish(last)
    value = s3[:, pl.ds(pl.multiple_of(at.z * width, 128), width)].astype(F32)
    for s in range(1, depth):
        value = value + rz[s - 1].astype(F32)
    total[...] = value


def scatter_buffers(d, depth):
    half, width = d // 2, d // depth
    return [
        pltpu.VMEM((2, 32, d), BF), pltpu.VMEM((2, 32, d), BF), pltpu.VMEM((32, half), BF),
        pltpu.VMEM((32, half), BF), pltpu.VMEM((2, 16, half), BF), pltpu.VMEM((2, 16, half), BF),
        pltpu.VMEM((16, half), BF), pltpu.VMEM((16, half), BF), pltpu.VMEM((16, d), BF),
        pltpu.VMEM((depth - 1, 16, width), BF),
    ]


def share_stats(at, wires, sums, out, inbox):
    lane = lax.broadcasted_iota(jnp.int32, (16, 128), 1)
    packed = jnp.zeros((16, 128), F32)
    for i, value in enumerate(sums):
        packed = jnp.where(lane == i, value, packed)
    out[...] = packed
    finish([wires.start(out, inbox.at[s - 1], at.z_peer(s)) for s in range(1, at.depth)])
    for s in range(1, at.depth):
        packed = packed + inbox[s - 1]
    return [packed[:, i : i + 1] for i in range(len(sums))]


def row_sum(value):
    return jnp.sum(value, axis=-1, keepdims=True)


def run(steps, work=()):
    work = iter(work)
    for _ in steps:
        next(work, None)


def middle(at, wires, total, stats, inbox, d, clean, answers, unembed, post_gain, final_gain):
    width = total.shape[1]
    rows = rows16((at.mp * 2 + at.x) * 16)
    columns = pl.ds(pl.multiple_of(at.z * width, 128), width)
    m = total[...]
    s = clean[rows, columns].astype(F32)
    pg = post_gain[:, columns]
    ids = answers[rows, :]
    candidate = lax.broadcasted_iota(jnp.int32, (16, unembed.shape[0]), 1)
    selector = (
        jnp.where(candidate == ids[:, 0:1], 1.0, 0.0) - jnp.where(candidate == ids[:, 1:2], 1.0, 0.0)
    ).astype(BF)
    direction = jnp.dot(selector, unembed[:, columns], preferred_element_type=F32)
    weighted = final_gain[:, columns] * direction
    mg = m * pg
    sums = [row_sum(m * m), row_sum(s * s), row_sum(s * mg), row_sum(mg * mg), row_sum(weighted * s), row_sum(weighted * mg)]
    mm, ss, smg, mgmg, ws, wmg = [v * (1.0 / d) for v in share_stats(at, wires, sums, stats, inbox)]
    inv_post = lax.rsqrt(mm + epsilon)
    inv_final = lax.rsqrt(ss + 2.0 * inv_post * smg + inv_post * inv_post * mgmg + epsilon)
    output = s + mg * inv_post
    lean = (inv_final * inv_final * inv_final) * (ws + inv_post * wmg)
    grad_output = inv_final * weighted - output * lean
    pull = inv_final * wmg - lean * (smg + inv_post * mgmg)
    grad_mlp = inv_post * (pg * grad_output) - m * (inv_post * inv_post * inv_post) * pull
    return grad_output, grad_mlp, ss


def last_grad(at, wires, total, stats, inbox, d, clean, pre_gain, grad_output, ss):
    width = total.shape[1]
    rows = rows16((at.mp * 2 + at.x) * 16)
    columns = pl.ds(pl.multiple_of(at.z * width, 128), width)
    s = clean[rows, columns].astype(F32)
    pre_grad = pre_gain[:, columns] * total[...]
    inv_pre = lax.rsqrt(ss + epsilon)
    (ps,) = share_stats(at, wires, [row_sum(pre_grad * s)], stats, inbox)
    return grad_output + inv_pre * pre_grad - s * (inv_pre * inv_pre * inv_pre) * (ps * (1.0 / d))


def whole_kernel(
    depth, pieces, own_clean, own_corrupt, target, answers, gains, b_enc, unembed_hbm, wg_hbm, wu_hbm, wd_hbm, we_hbm, wl_hbm, out,
    send, recv, load, wg, wu, wd, we, wl, unembed, buf0, buf1, xs, normed, gate_pre, up, hidden, grad_gate, grad_up,
    part, grads, change, kept, total, stats, inbox, own, *bufs,
):
    d, units = wg.shape
    latents = out.shape[1]
    rows = normed.shape[0]
    width = d // depth
    tile = we.shape[2]
    first = latents // 2
    pre_gain, post_gain, final_gain = gains.at[0:1], gains.at[1:2], gains.at[2:3]
    loads = [
        pltpu.make_async_copy(wg_hbm, wg, load.at[0]),
        pltpu.make_async_copy(wu_hbm, wu, load.at[1]),
        pltpu.make_async_copy(wd_hbm, wd, load.at[2]),
        pltpu.make_async_copy(unembed_hbm, unembed, load.at[3]),
        pltpu.make_async_copy(wl_hbm.at[first:latents], wl, load.at[4]),
    ]
    low = pltpu.make_async_copy(wl_hbm.at[0:first], wd.at[0:first], load.at[5])
    count = latents // tile

    def piece(p):
        return pltpu.make_async_copy(we_hbm.at[:, p * tile : (p + 1) * tile], we.at[p % 2], load.at[6 + p % 2])

    for copy in loads[:4]:
        copy.start()
    at = Place(depth)
    at.greet()
    wires = Wires(send, recv)
    run(gather_blocks(at, wires, own_clean, buf0))
    piece(0).start()
    piece(1).start()
    loads[4].start()
    side = gather_blocks(at, wires, own_corrupt, buf1)
    next(side, None)

    def arrange(buf, base):
        place = lax.broadcasted_iota(jnp.int32, (rows, rows * pieces), 1)
        for s in range(depth):
            pick = jnp.where(place == target[...] + s, 1.0, 0.0).astype(BF)
            xs[base : base + rows, s * width : (s + 1) * width] = jnp.dot(pick, buf[...], preferred_element_type=F32).astype(BF)

    arrange(buf0, 0)

    @pl.loop(0, rows // 16)
    def _(i):
        span = rows16(i * 16)
        stream = xs[span, :].astype(F32)
        inv_pre = lax.rsqrt(row_sum(stream * stream) * (1.0 / d) + epsilon)
        normed[span, :] = (stream * inv_pre * pre_gain[...]).astype(BF)

    next(side, None)
    loads[0].wait()
    loads[1].wait()
    cuts = [(a, min(a + 256, units)) for a in range(0, units, 256)]
    for n, (a, b) in enumerate(cuts):
        gate = jnp.dot(normed[...], wg[:, a:b], preferred_element_type=F32)
        lift = jnp.dot(normed[...], wu[:, a:b], preferred_element_type=F32)
        gate_pre[:, a:b] = gate
        up[:, a:b] = lift
        hidden[:, a:b] = (gelu_tanh(gate) * lift).astype(BF)
        if n % 2 == 1:
            next(side, None)
    for _ in side:
        pass
    loads[2].wait()
    def forward(low_quarter, high_quarter):
        @pl.loop(d // 256 * low_quarter // 4, d // 256 * high_quarter // 4)
        def _(i):
            span = pl.ds(pl.multiple_of(i * 256, 256), 256)
            part[:, span] = jnp.dot(hidden[...], wd[:, span], preferred_element_type=F32).astype(BF)

    def encode():
        for p in range(count):
            if p == 0:
                arrange(buf1, rows)
            piece(p).wait()
            span = slice(p * tile, (p + 1) * tile)
            code = jnp.dot(xs[...], we[p % 2], preferred_element_type=F32) + b_enc[:, span]
            code = jnp.maximum(code, 0.0)
            change[:, span] = code[:rows] - code[rows:]
            if p + 2 < count:
                piece(p + 2).start()
            yield

    clean = xs.at[0:rows]
    work = encode()
    run(scatter_sum(at, wires, part, bufs, total, forward), work)
    loads[3].wait()
    grad_output, grad_mlp, ss = middle(
        at, wires, total, stats, inbox, d, clean, answers, unembed, post_gain, final_gain
    )
    kept[...] = grad_output
    own[...] = grad_mlp.astype(BF)
    run(gather_rows(at, wires, own, grads), work)
    for a, b in cuts:
        grad_hidden = contract_last(grads[...], wd[a:b, :])
        gate = gate_pre[:, a:b]
        grad_gate[:, a:b] = (grad_hidden * up[:, a:b] * gelu_slope(gate)).astype(BF)
        grad_up[:, a:b] = (grad_hidden * gelu_tanh(gate)).astype(BF)
    low.start()

    def backward(low_quarter, high_quarter):
        @pl.loop(d // 256 * low_quarter // 4, d // 256 * high_quarter // 4)
        def _(i):
            span = pl.ds(pl.multiple_of(i * 256, 256), 256)
            value = contract_last(grad_gate[...], wg[span, :]) + contract_last(grad_up[...], wu[span, :])
            part[:, span] = value.astype(BF)

    run(scatter_sum(at, wires, part, bufs, total, backward), work)
    own[...] = last_grad(at, wires, total, stats, inbox, d, clean, pre_gain, kept[...], ss).astype(BF)
    run(gather_rows(at, wires, own, grads), work)
    for _ in work:
        pass
    low.wait()
    loads[4].wait()
    for p in range(count):
        source = wd if (p + 1) * tile <= first else wl
        base = p * tile % first
        projected = contract_last(grads[...], source[base : base + tile, :])
        span = slice(p * tile, (p + 1) * tile)
        out[:, span] = jnp.sum(change[:, span] * projected, axis=0, keepdims=True)


def staged(
    depth,
    resid_clean,
    resid_corrupt,
    answer_ids,
    unembed,
    pre_gain,
    post_gain,
    final_gain,
    w_gate,
    w_up,
    w_down,
    w_enc,
    b_enc,
    w_dec,
):
    own_rows, d = resid_clean.shape
    width = d // depth
    units = w_gate.shape[1]
    latents = w_enc.shape[1]
    rows = own_rows * depth * 8
    pieces = 16 // own_rows
    tile = 256
    token = np.arange(rows, dtype=np.int32)[:, None]
    device = token // own_rows
    x, z = device % 2, device // 2 % depth
    c, y = device // (2 * depth) % 2, device // (4 * depth)
    target = (((c * 2 + y) * 2 + x) * depth + z) * 16 + token % own_rows * pieces
    target = jnp.asarray(target.astype(np.int32))
    vmem = pl.BlockSpec(memory_space=pltpu.VMEM)
    hbm = pl.BlockSpec(memory_space=pl.ANY)
    scratch = [
        pltpu.SemaphoreType.DMA((80,)), pltpu.SemaphoreType.DMA((80,)), pltpu.SemaphoreType.DMA((8,)),
        pltpu.VMEM((d, units), BF), pltpu.VMEM((d, units), BF), pltpu.VMEM((units, d), BF),
        pltpu.VMEM((2, d, tile), BF), pltpu.VMEM((latents // 2, d), BF), pltpu.VMEM(unembed.shape, BF),
        pltpu.VMEM((rows * pieces, width), BF), pltpu.VMEM((rows * pieces, width), BF),
        pltpu.VMEM((2 * rows, d), BF), pltpu.VMEM((rows, d), BF),
        pltpu.VMEM((rows, units), F32), pltpu.VMEM((rows, units), F32), pltpu.VMEM((rows, units), BF),
        pltpu.VMEM((rows, units), BF), pltpu.VMEM((rows, units), BF),
        pltpu.VMEM((rows, d), BF), pltpu.VMEM((rows, d), BF), pltpu.VMEM((rows, latents), F32),
        pltpu.VMEM((16, width), F32), pltpu.VMEM((16, width), F32), pltpu.VMEM((16, 128), F32),
        pltpu.VMEM((depth - 1, 16, 128), F32), pltpu.VMEM((16, width), BF),
    ] + scatter_buffers(d, depth)
    return pl.pallas_call(
        functools.partial(whole_kernel, depth, pieces),
        out_shape=jax.ShapeDtypeStruct((1, latents), F32),
        in_specs=[vmem] * 6 + [hbm] * 6,
        out_specs=vmem,
        scratch_shapes=scratch,
        compiler_params=pltpu.CompilerParams(
            collective_id=0, has_side_effects=True, vmem_limit_bytes=67043328
        ),
    )(
        resid_clean.reshape(16, width), resid_corrupt.reshape(16, width), target, answer_ids,
        jnp.stack([pre_gain, post_gain, final_gain]), b_enc[None], unembed, w_gate, w_up, w_down, w_enc, w_dec,
    )


def fits(mesh, rows, d, units, latents):
    depth = mesh.shape["latent"] // 2
    return (
        mesh.shape["mp"] == 4 and depth >= 2 and rows == 128 and 16 * mesh.shape["latent"] * 4 == rows * depth
        and d % (128 * depth) == 0 and d % 512 == 0
        and rows == SEQ and units % 128 == 0 and latents % 512 == 0 and latents // 2 <= units
    )


def solution(mesh):
    def chosen(resid_clean, *rest):
        rows = resid_clean.shape[0] * mesh.shape["mp"] * mesh.shape["latent"]
        if fits(mesh, rows, resid_clean.shape[1], rest[6].shape[1], rest[9].shape[1]):
            return staged(mesh.shape["latent"] // 2, resid_clean, *rest)
        return local(resid_clean, *rest)

    return jax.shard_map(
        chosen,
        mesh=mesh,
        in_specs=(
            P(("mp", "latent"), None),
            P(("mp", "latent"), None),
            P(),
            P(),
            P(),
            P(),
            P(),
            P(None, ("mp", "latent")),
            P(None, ("mp", "latent")),
            P(("mp", "latent"), None),
            P(None, ("mp", "latent")),
            P(("mp", "latent")),
            P(("mp", "latent"), None),
        ),
        out_specs=P(None, ("mp", "latent")),
        check_vma=False,
    )
```
